32 devices in a mesh: rep: 2 (over x), shard: 16 (over z, y, core).
Axes of the slice: x: 2, y: 2, z: 4, core: 2. Of those that a mesh axis runs over, the one named last changes fastest.
Arguments:
- layer_input: bfloat16 [32, 256, 768], P(('rep', 'shard')), may hold values from -20 to 20, as said below
- lengths: int32 [32], P(('rep', 'shard')), may hold values from 1 to 256, 5120 in all
- cotangent: bfloat16 [32, 256, 768], P(('rep', 'shard')), may hold values from -6 to 6
- query_weight: bfloat16 [768, 768], P('shard'), may hold values from -0.21875 to 0.21875
- key_weight: bfloat16 [768, 768], P('shard'), may hold values from -0.21875 to 0.21875
- value_weight: bfloat16 [768, 768], P('shard'), may hold values from -0.21875 to 0.21875
- output_weight: bfloat16 [768, 768], P('shard'), may hold values from -1.25 to 1.25
- query_bias: bfloat16 [768], P('shard'), may hold values from -3 to 3
- value_bias: bfloat16 [768], P('shard'), may hold values from -3 to 3
- output_bias: bfloat16 [768], P('shard'), may hold values from -3 to 3
- first_gain: bfloat16 [768], P('shard'), may hold values from 0.5 to 1.5
- first_shift: bfloat16 [768], P('shard'), may hold values from -3 to 3
- inner_weight: bfloat16 [768, 3072], P('shard'), may hold values from -0.21875 to 0.21875
- inner_bias: bfloat16 [3072], P('shard'), may hold values from -3 to 3
- outer_weight: bfloat16 [3072, 768], P('shard'), may hold values from -0.109375 to 0.109375
- outer_bias: bfloat16 [768], P('shard'), may hold values from -3 to 3
- second_gain: bfloat16 [768], P('shard'), may hold values from 0.5 to 1.5
- second_shift: bfloat16 [768], P('shard'), may hold values from -3 to 3
Outputs:
- block_output: bfloat16 [32, 256, 768], P(('rep', 'shard'))
- input_grad: float32 [32, 256, 768], P(('rep', 'shard'))
- grad_query_weight: float32 [768, 768], P('shard')
- grad_key_weight: float32 [768, 768], P('shard')
- grad_value_weight: float32 [768, 768], P('shard')
- grad_output_weight: float32 [768, 768], P('shard')
- grad_query_bias: float32 [768], P('shard')
- grad_value_bias: float32 [768], P('shard')
- grad_output_bias: float32 [768], P('shard')
- grad_first_gain: float32 [768], P('shard')
- grad_first_shift: float32 [768], P('shard')
- grad_inner_weight: float32 [768, 3072], P('shard')
- grad_inner_bias: float32 [3072], P('shard')
- grad_outer_weight: float32 [3072, 768], P('shard')
- grad_outer_bias: float32 [768], P('shard')
- grad_second_gain: float32 [768], P('shard')
- grad_second_shift: float32 [768], P('shard')
The draws below stay inside these ranges and needn't reach their ends.
Inputs may be any that keep to these rules, and one draw needn't show every extreme that they name: `lengths`: positions at or after a sequence's length are padding: no query attends to them. The longest sequence has exactly 256 valid positions. `layer_input`: the layer's input.
All inputs are finite; a program needn't handle non-finite values. No bound on the sum of `lengths` on one device may be relied on, other than what follows from the above.
Results may differ from the reference program's by a relative error of at most 0.019.
The reference program's roundings to bfloat16 on the way (of `attend`, `context`, `first_low`, `active`, `second_low`, `inner_low` and `score_low`) count: a program that leaves them out, or rounds other values in their place, can miss the bound.
Values may be sent and summed in bfloat16 or wider, within the bound.
No kernel may reach another device: no remote copies, remote signals or barrier semaphores. Data moves between devices by JAX's collectives and lax.ppermute only.
A program may use at most 128 MiB of HBM per device.

```python
import math
import jax
import jax.numpy as jnp
import numpy as np
from jax import lax

D = 768
HEAD_DIM = 64
FF = 3072
SEQ_LEN = 256
SEQS = 32
TOKENS = 8192


def draw_layer_input(key, part):
    first_key = jax.random.fold_in(jax.random.fold_in(key, 17), 0)
    values = jnp.clip(jax.random.normal(first_key, (SEQS, SEQ_LEN, D), jnp.float32), -6.0, 6.0)
    return values.astype(jnp.bfloat16)


def shard_levels(rng, shape, cuts, low, top_value):
    gain, own = 1.0, jax.random.fold_in(rng, 6)
    for dim, parts in cuts:
        steps = jnp.exp(jax.random.uniform(jax.random.fold_in(own, dim), (parts,), jnp.float32, low / len(cuts), top_value / len(cuts)))
        gain = gain * jnp.repeat(steps, shape[dim] // parts).reshape([-1 if axis == dim else 1 for axis in range(len(shape))])
    return gain


def length_profile(number_of, total, bound, slope):
    loads = [(1 << 20) // math.isqrt(rank ** slope) + 1 for rank in range(2, number_of + 1)]
    spare, holding = total - bound - (number_of - 1), [1] * (number_of - 1)
    while spare > 0:
        movable = [i for i in range(number_of - 1) if holding[i] < bound]
        mass, left = sum([loads[i] for i in movable]), spare
        for i in movable:
            addition = min(bound - holding[i], max(1, left * loads[i] // mass), spare)
            holding[i] = holding[i] + addition
            spare = spare - addition
    return np.array([bound] + holding)


def uneven(stream_key, number_of, total, limit, lean):
    if number_of == 2:
        one = jax.random.randint(stream_key, (), max(1, total - limit), min(limit, total - 1) + 1)
        return jnp.stack([one, total - one])
    tallies = jnp.asarray(length_profile(number_of, total, limit, lean), jnp.int32)
    twos = (number_of - 1) // 2
    donor, taker = tallies[1:1 + 2 * twos:2], tallies[2:2 + 2 * twos:2]
    room = jnp.minimum(donor - 1, limit - taker)
    passed = jax.random.randint(jax.random.fold_in(stream_key, 1), (twos,), 0, 1 << 20) % (room + 1)
    tallies = tallies.at[1:1 + 2 * twos:2].set(donor - passed).at[2:2 + 2 * twos:2].set(taker + passed)
    return tallies[jax.random.permutation(jax.random.fold_in(stream_key, 2), number_of)]


def centred(rng, dims, scale, bound, cuts=(), held_as=jnp.bfloat16):
    entries = jax.random.normal(rng, dims, jnp.float32) * scale
    if len(cuts) > 0:
        entries = shard_levels(rng, dims, cuts, -0.22, 0.18) * entries
    return jnp.clip(entries, min=-bound, max=bound).astype(held_as)


def setup_inputs(seed: int = 0) -> dict:
    streams_of = jax.random.split(jax.random.key(seed), 19)
    return {
        "layer_input": draw_layer_input(jax.random.fold_in(streams_of[18], 71), 0),
        "lengths": uneven(streams_of[1], SEQS, SEQS * SEQ_LEN * 5 // 8, SEQ_LEN, 1).astype(jnp.int32),
        "cotangent": centred(streams_of[2], (SEQS, SEQ_LEN, D), 1.0, 6.0, ((0, 32),)),
        "query_weight": centred(streams_of[3], (D, D), D ** -0.5, 0.21875, ((0, 16),)),
        "key_weight": centred(streams_of[4], (D, D), D ** -0.5, 0.21875, ((0, 16),)),
        "value_weight": centred(streams_of[5], (D, D), D ** -0.5, 0.21875, ((0, 16),)),
        "output_weight": centred(streams_of[6], (D, D), (D // 32) ** -0.5, 1.25, ((0, 16),)),
        "query_bias": centred(streams_of[7], (D,), 0.5, 3.0, ((0, 16),)),
        "value_bias": centred(streams_of[8], (D,), 0.5, 3.0, ((0, 16),)),
        "output_bias": centred(streams_of[9], (D,), 0.5, 3.0, ((0, 16),)),
        "first_gain": jnp.clip(1.0 + 0.1 * jax.random.normal(streams_of[10], (D,), jnp.float32), 0.5, 1.5).astype(jnp.bfloat16),
        "first_shift": centred(streams_of[11], (D,), 0.5, 3.0, ((0, 16),)),
        "inner_weight": centred(streams_of[12], (D, FF), D ** -0.5, 0.21875, ((0, 16),)),
        "inner_bias": centred(streams_of[13], (FF,), 0.5, 3.0, ((0, 16),)),
        "outer_weight": centred(streams_of[14], (FF, D), FF ** -0.5, 0.109375, ((0, 16),)),
        "outer_bias": centred(streams_of[15], (D,), 0.5, 3.0, ((0, 16),)),
        "second_gain": jnp.clip(1.0 + 0.1 * jax.random.normal(streams_of[16], (D,), jnp.float32), 0.5, 1.5).astype(jnp.bfloat16),
        "second_shift": centred(streams_of[17], (D,), 0.5, 3.0, ((0, 16),)),
    }


EPSILON = 1e-06
NEG_FILL = -1000000000.0
ROOT_HALF = 0.7071067811865476
INV_ROOT_TAU = 0.3989422804014327

def matmul(left, right):
    return jnp.dot(left, right, preferred_element_type=jnp.float32)

def transpose_left(left, right):
    return jnp.dot(left.T, right, preferred_element_type=jnp.float32)

def transpose_right(left, right):
    return jnp.dot(left, right.T, preferred_element_type=jnp.float32)

def batched(form, left, right):
    return jnp.einsum(form, left.astype(jnp.float32), right.astype(jnp.float32))

def gelu_exact(values):
    return 0.5 * values * (1.0 + lax.erf(values * ROOT_HALF))

def gelu_slope(values):
    return 0.5 * (1.0 + lax.erf(values * ROOT_HALF)) + values * jnp.exp(-0.5 * values * values) * INV_ROOT_TAU

def norm_forward(hidden, norm_gain, norm_shift):
    center = hidden - lax.optimization_barrier(jnp.mean(hidden, axis=-1, keepdims=True))
    reciprocal = lax.rsqrt(lax.optimization_barrier(jnp.mean(center * center, axis=-1, keepdims=True)) + EPSILON)
    normed = center * reciprocal
    return (normed * norm_gain.astype(jnp.float32) + norm_shift.astype(jnp.float32), normed, reciprocal)

def norm_backward(upstream, normed, reciprocal, norm_gain):
    scaled = upstream * norm_gain.astype(jnp.float32)
    centered = scaled - lax.optimization_barrier(jnp.mean(scaled, axis=-1, keepdims=True)) - normed * lax.optimization_barrier(jnp.mean(scaled * normed, axis=-1, keepdims=True))
    return (centered * reciprocal, lax.optimization_barrier(jnp.sum(upstream * normed, axis=0)), lax.optimization_barrier(jnp.sum(upstream, axis=0)))

def masked_scores(query_rows, key_rows, key_valid, split_shape):
    scaled = batched('bqhe,bkhe->bhqk', query_rows.reshape(split_shape), key_rows.reshape(split_shape)) * HEAD_DIM ** (-0.5)
    return jnp.where(key_valid[:, None, None, :], scaled, NEG_FILL)

def attention_forward(token_rows, key_valid, params, split_shape):
    query_weight, key_weight, value_weight, output_weight, query_bias, value_bias, output_bias, first_gain, first_shift = params
    query_rows = (matmul(token_rows, query_weight) + query_bias.astype(jnp.float32)).astype(jnp.bfloat16)
    key_rows = matmul(token_rows, key_weight).astype(jnp.bfloat16)
    value_rows = (matmul(token_rows, value_weight) + value_bias.astype(jnp.float32)).astype(jnp.bfloat16)
    scores = masked_scores(query_rows, key_rows, key_valid, split_shape)
    highest = lax.optimization_barrier(jnp.max(scores, axis=-1, keepdims=True))
    log_total = highest + jnp.log(lax.optimization_barrier(jnp.sum(jnp.exp(scores - highest), axis=-1, keepdims=True)))
    attend = jnp.exp(scores - log_total).astype(jnp.bfloat16)
    context = batched('bhqk,bkhe->bqhe', attend, value_rows.reshape(split_shape)).astype(jnp.bfloat16).reshape(token_rows.shape)
    first_sum = token_rows.astype(jnp.float32) + matmul(context, output_weight) + output_bias.astype(jnp.float32)
    first_out, first_normed, first_recip = norm_forward(first_sum, first_gain, first_shift)
    return (query_rows, key_rows, value_rows, log_total, context, first_out, first_normed, first_recip)

def feedforward_forward(first_out, params):
    inner_weight, inner_bias, outer_weight, outer_bias, second_gain, second_shift = params
    first_low = first_out.astype(jnp.bfloat16)
    inner_pre = matmul(first_low, inner_weight) + inner_bias.astype(jnp.float32)
    active = gelu_exact(inner_pre).astype(jnp.bfloat16)
    second_sum = first_out + matmul(active, outer_weight) + outer_bias.astype(jnp.float32)
    block_rows, second_normed, second_recip = norm_forward(second_sum, second_gain, second_shift)
    return (first_low, inner_pre, active, second_normed, second_recip, block_rows.astype(jnp.bfloat16))

def feedforward_backward(upstream, stored, params):
    first_low, inner_pre, active, second_normed, second_recip = stored
    inner_weight, inner_bias, outer_weight, outer_bias, second_gain, second_shift = params
    grad_second, grad_gain, grad_shift = norm_backward(upstream, second_normed, second_recip, second_gain)
    second_low = grad_second.astype(jnp.bfloat16)
    grad_outer = transpose_left(active, second_low)
    grad_outer_bias = lax.optimization_barrier(jnp.sum(grad_second, axis=0))
    grad_inner_pre = transpose_right(second_low, outer_weight) * gelu_slope(inner_pre)
    inner_low = grad_inner_pre.astype(jnp.bfloat16)
    grad_inner = transpose_left(first_low, inner_low)
    grad_inner_bias = lax.optimization_barrier(jnp.sum(grad_inner_pre, axis=0))
    grad_first_out = transpose_right(inner_low, inner_weight) + grad_second
    return (grad_first_out, (grad_inner, grad_inner_bias, grad_outer, grad_outer_bias, grad_gain, grad_shift))

def attention_backward(grad_first_out, stored, params, token_rows, key_valid, split_shape):
    query_rows, key_rows, value_rows, log_total, context, first_normed, first_recip = stored
    query_weight, key_weight, value_weight, output_weight, query_bias, value_bias, output_bias, first_gain, first_shift = params
    grad_first, grad_gain, grad_shift = norm_backward(grad_first_out, first_normed, first_recip, first_gain)
    first_grad_low = grad_first.astype(jnp.bfloat16)
    grad_output = transpose_left(context, first_grad_low)
    grad_output_bias = lax.optimization_barrier(jnp.sum(grad_first, axis=0))
    context_low = transpose_right(first_grad_low, output_weight).astype(jnp.bfloat16)
    scores = masked_scores(query_rows, key_rows, key_valid, split_shape)
    attention = jnp.exp(scores - log_total)
    attend = attention.astype(jnp.bfloat16)
    context_split = context_low.reshape(split_shape)
    grad_values = batched('bhqk,bqhe->bkhe', attend, context_split).reshape(token_rows.shape)
    grad_attend = batched('bqhe,bkhe->bhqk', context_split, value_rows.reshape(split_shape))
    across = batched('bqhe,bqhe->bhq', context_split, context.reshape(split_shape))
    score_low = (attention * (grad_attend - across[..., None]) * HEAD_DIM ** (-0.5)).astype(jnp.bfloat16)
    grad_query = batched('bhqk,bkhe->bqhe', score_low, key_rows.reshape(split_shape)).reshape(token_rows.shape)
    grad_keys = batched('bhqk,bqhe->bkhe', score_low, query_rows.reshape(split_shape)).reshape(token_rows.shape)
    query_low = grad_query.astype(jnp.bfloat16)
    key_low = grad_keys.astype(jnp.bfloat16)
    value_low = grad_values.astype(jnp.bfloat16)
    input_grad = grad_first + transpose_right(query_low, query_weight) + transpose_right(key_low, key_weight) + transpose_right(value_low, value_weight)
    gradients = (transpose_left(token_rows, query_low), transpose_left(token_rows, key_low), transpose_left(token_rows, value_low), grad_output, lax.optimization_barrier(jnp.sum(grad_query, axis=0)), lax.optimization_barrier(jnp.sum(grad_values, axis=0)), grad_output_bias, grad_gain, grad_shift)
    return (input_grad, gradients)

def layer(inputs, lengths, cotangent, params):
    sequence_count, position_count, model_width = inputs.shape
    split_shape = (sequence_count, position_count, model_width // HEAD_DIM, HEAD_DIM)
    token_rows = inputs.reshape(-1, model_width)
    key_valid = lax.broadcasted_iota(jnp.int32, (sequence_count, position_count), 1) < lengths.astype(jnp.int32)[:, None]
    first_params = params[:9]
    second_params = params[9:]
    query_rows, key_rows, value_rows, log_total, context, first_out, first_normed, first_recip = attention_forward(token_rows, key_valid, first_params, split_shape)
    first_low, inner_pre, active, second_normed, second_recip, block_rows = feedforward_forward(first_out, second_params)
    upstream = cotangent.reshape(-1, model_width).astype(jnp.float32)
    grad_first_out, second_grads = feedforward_backward(upstream, (first_low, inner_pre, active, second_normed, second_recip), second_params)
    input_grad, first_grads = attention_backward(grad_first_out, (query_rows, key_rows, value_rows, log_total, context, first_normed, first_recip), first_params, token_rows, key_valid, split_shape)
    return (block_rows.reshape(inputs.shape), input_grad.reshape(inputs.shape), first_grads + second_grads)

def reference(layer_input, lengths, cotangent, query_weight, key_weight, value_weight, output_weight, query_bias, value_bias, output_bias, first_gain, first_shift, inner_weight, inner_bias, outer_weight, outer_bias, second_gain, second_shift):
    params = (query_weight, key_weight, value_weight, output_weight, query_bias, value_bias, output_bias, first_gain, first_shift, inner_weight, inner_bias, outer_weight, outer_bias, second_gain, second_shift)
    block_count = math.gcd(SEQS, max(1, 4096 // SEQ_LEN))
    steps_count = SEQS // block_count
    inputs = layer_input.reshape(steps_count, block_count, SEQ_LEN, D)
    lengths_blocks = lengths.reshape(steps_count, block_count)
    cotangent_blocks = cotangent.reshape(steps_count, block_count, SEQ_LEN, D)

    def advance(carry, pieces):
        block_in, block_lengths, block_cotangent = pieces
        block_out, block_grad, gradients = layer(block_in, block_lengths, block_cotangent, params)
        return (jax.tree.map(jnp.add, carry, gradients), (block_out, block_grad))
    initial = tuple((jnp.zeros(weight.shape, jnp.float32) for weight in params))
    totals, stacked = lax.scan(advance, initial, (inputs, lengths_blocks, cotangent_blocks))
    block_output = stacked[0].reshape(SEQS, SEQ_LEN, D)
    input_grad = stacked[1].reshape(SEQS, SEQ_LEN, D)
    factor = float(TOKENS) ** (-0.5)
    scaled = [total * factor for total in totals]
    return (block_output, input_grad, scaled[0], scaled[1], scaled[2], scaled[3], scaled[4], scaled[5], scaled[6], scaled[7], scaled[8], scaled[9], scaled[10], scaled[11], scaled[12], scaled[13], scaled[14])
```

```python
import jax
import jax.numpy as jnp
from jax import lax
from jax.sharding import PartitionSpec as P

HEAD_DIM = 64


EPSILON = 1e-06
NEG_FILL = -1000000000.0
ROOT_HALF = 0.7071067811865476
INV_ROOT_TAU = 0.3989422804014327


def matmul(left, right):
    return jnp.dot(left, right, preferred_element_type=jnp.float32)


def transpose_left(left, right):
    return lax.dot_general(
        left, right, (((0,), (0,)), ((), ())), preferred_element_type=jnp.float32
    )


def transpose_right(left, right):
    return lax.dot_general(
        left, right, (((1,), (1,)), ((), ())), preferred_element_type=jnp.float32
    )


def batched(form, left, right):
    return jnp.einsum(form, left, right, preferred_element_type=jnp.float32)


def gelu_exact(values):
    return 0.5 * values * (1.0 + lax.erf(values * ROOT_HALF))


def gelu_slope(values):
    return (
        0.5 * (1.0 + lax.erf(values * ROOT_HALF))
        + values * jnp.exp(-0.5 * values * values) * INV_ROOT_TAU
    )


def norm_forward(hidden, norm_gain, norm_shift):
    center = hidden - jnp.mean(hidden, axis=-1, keepdims=True)
    reciprocal = lax.rsqrt(jnp.mean(center * center, axis=-1, keepdims=True) + EPSILON)
    normed = center * reciprocal
    return (
        normed * norm_gain.astype(jnp.float32) + norm_shift.astype(jnp.float32),
        normed,
        reciprocal,
    )


def norm_backward(upstream, normed, reciprocal, norm_gain):
    scaled = upstream * norm_gain.astype(jnp.float32)
    centered = (
        scaled
        - jnp.mean(scaled, axis=-1, keepdims=True)
        - normed * jnp.mean(scaled * normed, axis=-1, keepdims=True)
    )
    return (centered * reciprocal, jnp.sum(upstream * normed, axis=0), jnp.sum(upstream, axis=0))


def masked_scores(query_rows, key_rows, key_valid, split_shape):
    scaled = batched(
        "bqhe,bkhe->bhqk", query_rows.reshape(split_shape), key_rows.reshape(split_shape)
    ) * HEAD_DIM ** (-0.5)
    return jnp.where(key_valid[:, None, None, :], scaled, NEG_FILL)


def attention_forward(token_rows, key_valid, params, split_shape):
    (
        query_weight,
        key_weight,
        value_weight,
        output_weight,
        query_bias,
        value_bias,
        output_bias,
        first_gain,
        first_shift,
    ) = params
    query_rows = (matmul(token_rows, query_weight) + query_bias.astype(jnp.float32)).astype(
        jnp.bfloat16
    )
    key_rows = matmul(token_rows, key_weight).astype(jnp.bfloat16)
    value_rows = (matmul(token_rows, value_weight) + value_bias.astype(jnp.float32)).astype(
        jnp.bfloat16
    )
    scores = masked_scores(query_rows, key_rows, key_valid, split_shape)
    highest = jnp.max(scores, axis=-1, keepdims=True)
    log_total = highest + jnp.log(jnp.sum(jnp.exp(scores - highest), axis=-1, keepdims=True))
    attend = jnp.exp(scores - log_total).astype(jnp.bfloat16)
    context = (
        batched("bhqk,bkhe->bqhe", attend, value_rows.reshape(split_shape))
        .astype(jnp.bfloat16)
        .reshape(token_rows.shape)
    )
    first_sum = (
        token_rows.astype(jnp.float32)
        + matmul(context, output_weight)
        + output_bias.astype(jnp.float32)
    )
    first_out, first_normed, first_recip = norm_forward(first_sum, first_gain, first_shift)
    return (
        query_rows,
        key_rows,
        value_rows,
        log_total,
        context,
        first_out,
        first_normed,
        first_recip,
    )


def feedforward_forward(first_out, params):
    inner_weight, inner_bias, outer_weight, outer_bias, second_gain, second_shift = params
    first_low = first_out.astype(jnp.bfloat16)
    inner_pre = matmul(first_low, inner_weight) + inner_bias.astype(jnp.float32)
    active = gelu_exact(inner_pre).astype(jnp.bfloat16)
    second_sum = first_out + matmul(active, outer_weight) + outer_bias.astype(jnp.float32)
    block_rows, second_normed, second_recip = norm_forward(second_sum, second_gain, second_shift)
    return (
        first_low,
        inner_pre,
        active,
        second_normed,
        second_recip,
        block_rows.astype(jnp.bfloat16),
    )


def feedforward_backward(upstream, stored, params):
    first_low, inner_pre, active, second_normed, second_recip = stored
    inner_weight, inner_bias, outer_weight, outer_bias, second_gain, second_shift = params
    grad_second, grad_gain, grad_shift = norm_backward(
        upstream, second_normed, second_recip, second_gain
    )
    second_low = grad_second.astype(jnp.bfloat16)
    grad_outer = transpose_left(active, second_low)
    grad_outer_bias = jnp.sum(grad_second, axis=0)
    grad_inner_pre = transpose_right(second_low, outer_weight) * gelu_slope(inner_pre)
    inner_low = grad_inner_pre.astype(jnp.bfloat16)
    grad_inner = transpose_left(first_low, inner_low)
    grad_inner_bias = jnp.sum(grad_inner_pre, axis=0)
    grad_first_out = transpose_right(inner_low, inner_weight) + grad_second
    return (
        grad_first_out,
        (grad_inner, grad_inner_bias, grad_outer, grad_outer_bias, grad_gain, grad_shift),
    )


def attention_backward(grad_first_out, stored, params, token_rows, key_valid, split_shape):
    query_rows, key_rows, value_rows, log_total, context, first_normed, first_recip = stored
    (
        query_weight,
        key_weight,
        value_weight,
        output_weight,
        query_bias,
        value_bias,
        output_bias,
        first_gain,
        first_shift,
    ) = params
    grad_first, grad_gain, grad_shift = norm_backward(
        grad_first_out, first_normed, first_recip, first_gain
    )
    first_grad_low = grad_first.astype(jnp.bfloat16)
    grad_output = transpose_left(context, first_grad_low)
    grad_output_bias = jnp.sum(grad_first, axis=0)
    context_low = transpose_right(first_grad_low, output_weight).astype(jnp.bfloat16)
    scores = masked_scores(query_rows, key_rows, key_valid, split_shape)
    attention = jnp.exp(scores - log_total)
    attend = attention.astype(jnp.bfloat16)
    context_split = context_low.reshape(split_shape)
    grad_values = batched("bhqk,bqhe->bkhe", attend, context_split).reshape(token_rows.shape)
    grad_attend = batched("bqhe,bkhe->bhqk", context_split, value_rows.reshape(split_shape))
    across = batched("bqhe,bqhe->bhq", context_split, context.reshape(split_shape))
    score_low = (attention * (grad_attend - across[..., None]) * HEAD_DIM ** (-0.5)).astype(
        jnp.bfloat16
    )
    grad_query = batched("bhqk,bkhe->bqhe", score_low, key_rows.reshape(split_shape)).reshape(
        token_rows.shape
    )
    grad_keys = batched("bhqk,bqhe->bkhe", score_low, query_rows.reshape(split_shape)).reshape(
        token_rows.shape
    )
    query_low = grad_query.astype(jnp.bfloat16)
    key_low = grad_keys.astype(jnp.bfloat16)
    value_low = grad_values.astype(jnp.bfloat16)
    input_grad = (
        grad_first
        + transpose_right(query_low, query_weight)
        + transpose_right(key_low, key_weight)
        + transpose_right(value_low, value_weight)
    )
    gradients = (
        transpose_left(token_rows, query_low),
        transpose_left(token_rows, key_low),
        transpose_left(token_rows, value_low),
        grad_output,
        jnp.sum(grad_query, axis=0),
        jnp.sum(grad_values, axis=0),
        grad_output_bias,
        grad_gain,
        grad_shift,
    )
    return (input_grad, gradients)


def swap(values, axis, bit):
    pairs = [(i, i ^ bit) for i in range(lax.axis_size(axis))]
    return lax.ppermute(values, axis, pairs)


def has_bit(axis, bit):
    return (lax.axis_index(axis) & bit) != 0


def bits_of(axis):
    return [1 << k for k in range(lax.axis_size(axis).bit_length() - 1)]


def gather(block):
    bits = bits_of("shard")
    rows, columns = block.shape
    seen = []
    for bit in bits[2:] + bits[:2][::-1]:
        other = swap(block, "shard", bit)
        before = 1 << sum(1 for past in seen if past > bit)
        shape = (before, 1, block.shape[0] // before, columns)
        mine, other = block.reshape(shape), other.reshape(shape)
        high = has_bit("shard", bit)
        block = jnp.concatenate(
            [jnp.where(high, other, mine), jnp.where(high, mine, other)], axis=1
        ).reshape(-1, columns)
        seen.append(bit)
    return block


def halve(total, axis, bit, before):
    columns = total.shape[-1]
    mine = has_bit(axis, bit).astype(jnp.int32)
    total = total.reshape(before, 2, -1, columns)
    send = lax.dynamic_index_in_dim(total, 1 - mine, 1, keepdims=False)
    keep = lax.dynamic_index_in_dim(total, mine, 1, keepdims=False)
    send, keep = send.reshape(-1, columns), keep.reshape(-1, columns)
    other = swap(send.astype(jnp.bfloat16), axis, bit)
    return keep.astype(jnp.float32) + other.astype(jnp.float32)


def scatter(total, rep_first):
    bits, reps = bits_of("shard"), bits_of("rep")
    columns = total.shape[-1]
    left = [("shard", bit) for bit in reversed(bits)] + [("rep", bit) for bit in reversed(reps)]
    across = [("rep", bit) for bit in reps]
    near = [("shard", bit) for bit in bits[1:2]]
    order = [("shard", bits[0])]
    order += across + near if rep_first else near + across
    order += [("shard", bit) for bit in reversed(bits[2:])]
    for step in order:
        place = left.index(step)
        total = halve(total, step[0], step[1], 1 << place)
        left.pop(place)
    for bit in reps:
        other = swap(total.astype(jnp.bfloat16), "rep", bit).astype(jnp.float32)
        high = has_bit("rep", bit)
        total = jnp.concatenate(
            [jnp.where(high, other, total), jnp.where(high, total, other)], axis=0
        )
    return total


def body(
    layer_input,
    lengths,
    cotangent,
    query_weight,
    key_weight,
    value_weight,
    output_weight,
    query_bias,
    value_bias,
    output_bias,
    first_gain,
    first_shift,
    inner_weight,
    inner_bias,
    outer_weight,
    outer_bias,
    second_gain,
    second_shift,
):
    sequence_count, position_count, model_width = layer_input.shape
    split_shape = (sequence_count, position_count, model_width // HEAD_DIM, HEAD_DIM)
    token_rows = layer_input.reshape(-1, model_width)
    key_valid = (
        lax.broadcasted_iota(jnp.int32, (sequence_count, position_count), 1) < lengths[:, None]
    )
    part = query_weight.shape[0]
    shards = lax.axis_size("shard")
    spread = inner_bias.shape[0] // part
    vectors = [
        query_bias,
        value_bias,
        output_bias,
        first_gain,
        first_shift,
        outer_bias,
        second_gain,
        second_shift,
    ]
    table = jnp.concatenate(
        [jnp.stack(vectors), inner_bias.reshape(spread, part)], axis=0
    )
    table = jnp.pad(table.T, ((0, 0), (0, 128 - table.shape[0])))
    attention_block = jnp.concatenate(
        [query_weight, key_weight, value_weight, output_weight, table], axis=1
    )
    attention_all = gather(attention_block)
    inner_all = gather(inner_weight)
    outer_all = gather(outer_weight)
    weights = [attention_all[:, i * model_width : (i + 1) * model_width] for i in range(4)]
    rows = attention_all[:, 4 * model_width :].T
    full = [rows[i] for i in range(8)]
    inner_bias_all = (
        rows[8 : 8 + spread].reshape(spread, shards, part).transpose(1, 0, 2).reshape(-1)
    )
    first_params = tuple(weights) + (full[0], full[1], full[2], full[3], full[4])
    second_params = (inner_all, inner_bias_all, outer_all, full[5], full[6], full[7])
    query_rows, key_rows, value_rows, log_total, context, first_out, first_normed, first_recip = (
        attention_forward(token_rows, key_valid, first_params, split_shape)
    )
    first_low, inner_pre, active, second_normed, second_recip, block_rows = feedforward_forward(
        first_out, second_params
    )
    upstream = cotangent.reshape(-1, model_width).astype(jnp.float32)
    grad_first_out, second_grads = feedforward_backward(
        upstream, (first_low, inner_pre, active, second_normed, second_recip), second_params
    )
    (
        grad_inner,
        grad_inner_bias,
        grad_outer,
        grad_outer_bias,
        grad_second_gain,
        grad_second_shift,
    ) = second_grads
    own_outer = scatter(grad_outer, True)
    own_inner = scatter(grad_inner, False)
    input_grad, first_grads = attention_backward(
        grad_first_out,
        (query_rows, key_rows, value_rows, log_total, context, first_normed, first_recip),
        first_params,
        token_rows,
        key_valid,
        split_shape,
    )
    grad_rows = jnp.concatenate(
        [
            jnp.stack(
                list(first_grads[4:9]) + [grad_outer_bias, grad_second_gain, grad_second_shift]
            ),
            grad_inner_bias.reshape(shards, spread, part)
            .transpose(1, 0, 2)
            .reshape(spread, model_width),
        ],
        axis=0,
    )
    grad_table = jnp.pad(grad_rows.T, ((0, 0), (0, 128 - grad_rows.shape[0])))
    grad_block = jnp.concatenate(list(first_grads[:4]) + [grad_table], axis=1)
    own_block = scatter(grad_block, False)
    factor = float(token_rows.shape[0] * lax.axis_size("rep") * shards) ** (-0.5)
    own_block = own_block * factor
    own = [own_block[:, i * model_width : (i + 1) * model_width] for i in range(4)]
    own_rows = own_block[:, 4 * model_width :].T
    return (
        block_rows.reshape(layer_input.shape),
        input_grad.reshape(layer_input.shape),
        own[0],
        own[1],
        own[2],
        own[3],
        own_rows[0],
        own_rows[1],
        own_rows[2],
        own_rows[3],
        own_rows[4],
        own_inner * factor,
        own_rows[8 : 8 + spread].reshape(-1),
        own_outer * factor,
        own_rows[5],
        own_rows[6],
        own_rows[7],
    )


def solution(mesh):
    placed = (
        P(("rep", "shard"), None, None),
        P(("rep", "shard")),
        P(("rep", "shard"), None, None),
        P("shard", None),
        P("shard", None),
        P("shard", None),
        P("shard", None),
        P("shard"),
        P("shard"),
        P("shard"),
        P("shard"),
        P("shard"),
        P("shard", None),
        P("shard"),
        P("shard", None),
        P("shard"),
        P("shard"),
        P("shard"),
    )
    return jax.shard_map(
        body,
        mesh=mesh,
        in_specs=placed,
        out_specs=(
            P(("rep", "shard"), None, None),
            P(("rep", "shard"), None, None),
            P("shard", None),
            P("shard", None),
            P("shard", None),
            P("shard", None),
            P("shard"),
            P("shard"),
            P("shard"),
            P("shard"),
            P("shard"),
            P("shard", None),
            P("shard"),
            P("shard", None),
            P("shard"),
            P("shard"),
            P("shard"),
        ),
        check_vma=False,
    )
```

```python
import functools

import jax
import jax.numpy as jnp
from jax import lax
from jax.experimental import pallas as pl
from jax.experimental.pallas import tpu as pltpu
from jax.sharding import PartitionSpec as P

HEAD_DIM = 64
LANES = 128


EPSILON = 1e-06
NEG_FILL = -1000000000.0
ROOT_HALF = 0.7071067811865476
INV_ROOT_TAU = 0.3989422804014327


def matmul(left, right):
    return jnp.dot(left, right, preferred_element_type=jnp.float32)


def transpose_left(left, right):
    return lax.dot_general(
        left, right, (((0,), (0,)), ((), ())), preferred_element_type=jnp.float32
    )


def transpose_right(left, right):
    return lax.dot_general(
        left, right, (((1,), (1,)), ((), ())), preferred_element_type=jnp.float32
    )


def row_mean(values):
    return jnp.mean(values, axis=-1, keepdims=True)


def norm_forward(hidden):
    center = hidden - row_mean(hidden)
    reciprocal = lax.rsqrt(row_mean(center * center) + EPSILON)
    return center * reciprocal, reciprocal


def norm_backward(upstream, normed, reciprocal, gain):
    scaled = upstream * gain
    return (scaled - row_mean(scaled) - normed * row_mean(scaled * normed)) * reciprocal


def column_sum(values):
    return jnp.sum(values, axis=0, keepdims=True)


def call(kernel, outs, *args, **options):
    smem = [pl.BlockSpec(memory_space=pltpu.SMEM)]
    vmem = [pl.BlockSpec(memory_space=pltpu.VMEM)]
    return pl.pallas_call(
        kernel,
        out_shape=[jax.ShapeDtypeStruct(shape, dtype) for shape, dtype in outs],
        in_specs=[smem[0] if a.dtype == jnp.int32 else vmem[0] for a in args],
        out_specs=vmem * len(outs),
        compiler_params=pltpu.CompilerParams(vmem_limit_bytes=60 << 20),
        **options,
    )(*args)


def attention_forward(
    length, x, w, query, key, value, context, attention, low, normed, recip, rows
):
    width = x.shape[1]
    table = w[:, 4 * width :].astype(jnp.float32).T
    rows[...] = table[: rows.shape[0]]
    query[...] = (matmul(x[...], w[:, :width]) + rows[0:1]).astype(jnp.bfloat16)
    key[...] = matmul(x[...], w[:, width : 2 * width]).astype(jnp.bfloat16)
    value[...] = (matmul(x[...], w[:, 2 * width : 3 * width]) + rows[1:2]).astype(jnp.bfloat16)
    count = x.shape[0]
    valid = lax.broadcasted_iota(jnp.int32, (count, count), 1) < length[0]
    lane = lax.broadcasted_iota(jnp.int32, (count, LANES), 1) // HEAD_DIM

    def pair(j, carry):
        at = pl.ds(pl.multiple_of(j * LANES, LANES), LANES)
        queries, keys, values = query[:, at], key[:, at], value[:, at]
        total = jnp.zeros((count, LANES), jnp.float32)
        for h in range(LANES // HEAD_DIM):
            mine = jnp.where(lane == h, queries, jnp.zeros_like(queries))
            scores = transpose_right(mine, keys) * HEAD_DIM ** (-0.5)
            scores = jnp.where(valid, scores, NEG_FILL)
            top = jnp.max(scores, axis=-1, keepdims=True)
            log_total = top + jnp.log(jnp.sum(jnp.exp(scores - top), axis=-1, keepdims=True))
            attend = jnp.exp(scores - log_total)
            first = pl.multiple_of((j * (LANES // HEAD_DIM) + h) * count, count)
            attention[pl.ds(first, count), :] = attend
            total = jnp.where(lane == h, matmul(attend.astype(jnp.bfloat16), values), total)
        context[:, at] = total.astype(jnp.bfloat16)
        return carry

    lax.fori_loop(0, width // LANES, pair, 0)
    first_sum = (
        x[...].astype(jnp.float32) + matmul(context[...], w[:, 3 * width : 4 * width]) + rows[2:3]
    )
    first_normed, first_recip = norm_forward(first_sum)
    normed[...] = first_normed
    recip[...] = jnp.broadcast_to(first_recip, recip.shape)
    low[...] = (first_normed * rows[3:4] + rows[4:5]).astype(jnp.bfloat16)


def inner_forward(low, w, bias, active, slope):
    chunk = 4 * LANES
    for start in range(0, w.shape[1], chunk):
        at = slice(start, start + chunk)
        pre = matmul(low[...], w[:, at]) + bias[:, at]
        half = 0.5 * (1.0 + lax.erf(pre * ROOT_HALF))
        active[:, at] = (pre * half).astype(jnp.bfloat16)
        slope[:, at] = half + pre * jnp.exp(-0.5 * pre * pre) * INV_ROOT_TAU


def outer_both(normed, rows, active, w, slope, upstream, block, grad, low, inner_low, sums, bias):
    first_out = normed[...] * rows[3:4] + rows[4:5]
    second_sum = first_out + matmul(active[...], w[...]) + rows[5:6]
    second_normed, second_recip = norm_forward(second_sum)
    block[...] = (second_normed * rows[6:7] + rows[7:8]).astype(jnp.bfloat16)
    above = upstream[...].astype(jnp.float32)
    grad_second = norm_backward(above, second_normed, second_recip, rows[6:7])
    grad[...] = grad_second
    low[...] = grad_second.astype(jnp.bfloat16)
    sums[...] = jnp.zeros_like(sums)
    sums[0:1] = column_sum(grad_second)
    sums[1:2] = column_sum(above * second_normed)
    sums[2:3] = column_sum(above)
    chunk = 4 * LANES
    for start in range(0, w.shape[0], chunk):
        at = slice(start, start + chunk)
        grad_pre = transpose_right(low[...], w[at, :]) * slope[:, at]
        inner_low[:, at] = grad_pre.astype(jnp.bfloat16)
        bias[:, at] = column_sum(grad_pre)


def attention_backward(
    inner_low,
    inner_w,
    grad_second,
    normed,
    recip,
    rows,
    w,
    query,
    key,
    value,
    context,
    attention,
    grads,
    input_grad,
    sums,
    context_low,
):
    count, width = normed.shape
    grad_out = transpose_right(inner_low[...], inner_w[...]) + grad_second[...]
    grad_first = norm_backward(grad_out, normed[...], recip[:, 0:1], rows[3:4])
    sums[...] = jnp.zeros_like(sums)
    sums[2:3] = column_sum(grad_first)
    sums[3:4] = column_sum(grad_out * normed[...])
    sums[4:5] = column_sum(grad_out)
    grads[3] = grad_first.astype(jnp.bfloat16)
    context_low[...] = transpose_right(grads[3], w[:, 3 * width : 4 * width]).astype(jnp.bfloat16)
    lane = lax.broadcasted_iota(jnp.int32, (count, LANES), 1) // HEAD_DIM

    def pair(j, carry):
        at = pl.ds(pl.multiple_of(j * LANES, LANES), LANES)
        queries, keys, values = query[:, at], key[:, at], value[:, at]
        above = context_low[:, at]
        both = above.astype(jnp.float32) * context[:, at].astype(jnp.float32)
        total = [jnp.zeros((count, LANES), jnp.float32)] * 3
        for h in range(LANES // HEAD_DIM):
            mine = lane == h
            first = pl.multiple_of((j * (LANES // HEAD_DIM) + h) * count, count)
            attend = attention[pl.ds(first, count), :]
            grad_attend = transpose_right(jnp.where(mine, above, jnp.zeros_like(above)), values)
            across = jnp.sum(jnp.where(mine, both, 0.0), axis=-1, keepdims=True)
            score = (attend * (grad_attend - across) * HEAD_DIM ** (-0.5)).astype(jnp.bfloat16)
            parts = [
                matmul(score, keys),
                transpose_left(score, queries),
                transpose_left(attend.astype(jnp.bfloat16), above),
            ]
            total = [jnp.where(mine, new, old) for new, old in zip(parts, total)]
        for i in range(3):
            grads[i, :, at] = total[i].astype(jnp.bfloat16)
        sums[0:1, at] = column_sum(total[0])
        sums[1:2, at] = column_sum(total[2])
        return carry

    lax.fori_loop(0, width // LANES, pair, 0)
    result = grad_first
    for i in range(3):
        result += transpose_right(grads[i], w[:, i * width : (i + 1) * width])
    input_grad[...] = result


def split_halves(core, block, scratch, send, keep, part, at):
    scratch[...] = block
    for i in range(block.shape[0] // (2 * part)):
        base = 2 * part * i
        theirs = pl.ds(pl.multiple_of(base + (1 - core) * part, 8), part)
        ours = pl.ds(pl.multiple_of(base + core * part, 8), part)
        send[i * part : (i + 1) * part, at] = scratch[theirs, :].astype(jnp.bfloat16)
        keep[i * part : (i + 1) * part, at] = scratch[ours, :]


def weight_grad(part, core, left, right, send, keep, scratch):
    total = transpose_left(left[...], right[...])
    split_halves(core[0], total, scratch, send, keep, part, slice(0, right.shape[1]))


def block_grad(part, core, x, context, grads, sums, more, bias, send, keep, scratch, thin):
    width = grads.shape[2]
    for i in range(4):
        left = context if i == 3 else x
        total = transpose_left(left[...], grads[i])
        at = slice(i * width, (i + 1) * width)
        split_halves(core[0], total, scratch, send, keep, part, at)
    table = jnp.concatenate([sums[...], more[...], bias[...]], axis=0)
    table = jnp.concatenate(
        [table, jnp.zeros((LANES - table.shape[0], table.shape[1]), jnp.float32)], axis=0
    )
    split_halves(
        core[0], table.T, thin, send, keep, part, slice(4 * width, 4 * width + LANES)
    )


def swap(values, axis, bit):
    pairs = [(i, i ^ bit) for i in range(lax.axis_size(axis))]
    return lax.ppermute(values, axis, pairs)


def has_bit(axis, bit):
    return (lax.axis_index(axis) & bit) != 0


def bits_of(axis):
    return [1 << k for k in range(lax.axis_size(axis).bit_length() - 1)]


def gather(block):
    bits = bits_of("shard")
    rows, columns = block.shape
    seen = []
    for bit in bits[::-1][:-2] + bits[:2][::-1]:
        other = swap(block, "shard", bit)
        before = 1 << sum(1 for past in seen if past > bit)
        shape = (before, 1, block.shape[0] // before, columns)
        mine, other = block.reshape(shape), other.reshape(shape)
        high = has_bit("shard", bit)
        block = jnp.concatenate(
            [jnp.where(high, other, mine), jnp.where(high, mine, other)], axis=1
        ).reshape(-1, columns)
        seen.append(bit)
    return block


def halve(total, axis, bit, before):
    columns = total.shape[-1]
    mine = has_bit(axis, bit).astype(jnp.int32)
    total = total.reshape(before, 2, -1, columns)
    send = lax.dynamic_index_in_dim(total, 1 - mine, 1, keepdims=False)
    keep = lax.dynamic_index_in_dim(total, mine, 1, keepdims=False)
    send, keep = send.reshape(-1, columns), keep.reshape(-1, columns)
    other = swap(send.astype(jnp.bfloat16), axis, bit)
    return keep.astype(jnp.float32) + other.astype(jnp.float32)


def scatter(total, rep_first):
    bits, reps = bits_of("shard"), bits_of("rep")
    columns = total.shape[-1]
    left = [("shard", bit) for bit in reversed(bits[1:])] + [("rep", bit) for bit in reversed(reps)]
    across = [("rep", bit) for bit in reps]
    near = [("shard", bit) for bit in bits[1:2]]
    order = across + near if rep_first else near + across
    order += [("shard", bit) for bit in bits[2:]]
    for step in order:
        place = left.index(step)
        total = halve(total, step[0], step[1], 1 << place)
        left.pop(place)
    for bit in reps:
        other = swap(total.astype(jnp.bfloat16), "rep", bit).astype(jnp.float32)
        high = has_bit("rep", bit)
        total = jnp.concatenate(
            [jnp.where(high, other, total), jnp.where(high, total, other)], axis=0
        )
    return total


def swap_halves(send, keep):
    other = swap(send, "shard", 1)
    return keep + other.astype(jnp.float32)


def grad_pair(left, right, part, core):
    count, rows = left.shape
    columns = right.shape[1]
    step, wide = 3 * LANES, 6 * LANES
    return pl.pallas_call(
        functools.partial(weight_grad, part),
        grid=(rows // step, columns // wide),
        in_specs=[
            pl.BlockSpec(memory_space=pltpu.SMEM),
            pl.BlockSpec((count, step), lambda i, j: (0, i)),
            pl.BlockSpec((count, wide), lambda i, j: (0, j)),
        ],
        out_specs=[pl.BlockSpec((step // 2, wide), lambda i, j: (i, j))] * 2,
        out_shape=[
            jax.ShapeDtypeStruct((rows // 2, columns), jnp.bfloat16),
            jax.ShapeDtypeStruct((rows // 2, columns), jnp.float32),
        ],
        scratch_shapes=[pltpu.VMEM((step, wide), jnp.float32)],
    )(core, left, right)


def grad_block(x, context, grads, sums, more, bias, part, core):
    count, width = x.shape
    step = 3 * LANES
    columns = 4 * width + LANES
    thin = pl.BlockSpec((8, step), lambda i: (0, i))
    return pl.pallas_call(
        functools.partial(block_grad, part),
        grid=(width // step,),
        in_specs=[
            pl.BlockSpec(memory_space=pltpu.SMEM),
            pl.BlockSpec((count, step), lambda i: (0, i)),
            pl.BlockSpec((count, step), lambda i: (0, i)),
            pl.BlockSpec((4, count, width), lambda i: (0, 0, 0)),
            thin,
            thin,
            thin,
        ],
        out_specs=[pl.BlockSpec((step // 2, columns), lambda i: (i, 0))] * 2,
        out_shape=[
            jax.ShapeDtypeStruct((width // 2, columns), jnp.bfloat16),
            jax.ShapeDtypeStruct((width // 2, columns), jnp.float32),
        ],
        scratch_shapes=[
            pltpu.VMEM((step, width), jnp.float32),
            pltpu.VMEM((step, LANES), jnp.float32),
        ],
    )(core, x, context, grads, sums, more, bias)


def body(
    layer_input,
    lengths,
    cotangent,
    query_weight,
    key_weight,
    value_weight,
    output_weight,
    query_bias,
    value_bias,
    output_bias,
    first_gain,
    first_shift,
    inner_weight,
    inner_bias,
    outer_weight,
    outer_bias,
    second_gain,
    second_shift,
):
    count, width = layer_input.shape[1:]
    x = layer_input.reshape(-1, width)
    part, hidden = query_weight.shape[0], inner_weight.shape[1]
    shards = lax.axis_size("shard")
    spread = inner_bias.shape[0] // part
    vectors = [
        query_bias,
        value_bias,
        output_bias,
        first_gain,
        first_shift,
        outer_bias,
        second_gain,
        second_shift,
    ]
    table = jnp.concatenate(
        [jnp.stack(vectors), inner_bias.reshape(spread, part)], axis=0
    )
    table = jnp.pad(table.T, ((0, 0), (0, LANES - table.shape[0])))
    attention_block = jnp.concatenate(
        [query_weight, key_weight, value_weight, output_weight, table], axis=1
    )
    w = gather(attention_block)
    inner_all = gather(inner_weight)
    outer_all = gather(outer_weight)
    low, full = jnp.bfloat16, jnp.float32
    heads = width // HEAD_DIM
    square = (count, width)
    query, key, value, context, attention, first_low, normed, recip, rows = call(
        attention_forward,
        [(square, low)] * 4
        + [((heads * count, count), full), (square, low), (square, full)]
        + [((count, LANES), full), ((16, width), full)],
        lengths,
        x,
        w,
    )
    bias = rows[8 : 8 + spread].reshape(spread, shards, part).transpose(1, 0, 2).reshape(1, -1)
    active, slope = call(
        inner_forward,
        [((count, hidden), low), ((count, hidden), full)],
        first_low,
        inner_all,
        bias,
    )
    block_rows, grad_second, second_low, inner_low, more, bias_sum = call(
        outer_both,
        [
            (square, low),
            (square, full),
            (square, low),
            ((count, hidden), low),
            ((8, width), full),
            ((1, hidden), full),
        ],
        normed,
        rows,
        active,
        outer_all,
        slope,
        cotangent.reshape(-1, width),
    )
    core = (lax.axis_index("shard") & 1).reshape(1)
    own_outer = scatter(swap_halves(*grad_pair(active, second_low, part * spread, core)), True)
    own_inner = scatter(swap_halves(*grad_pair(first_low, inner_low, part, core)), False)
    grads, input_grad, sums = call(
        attention_backward,
        [((4,) + square, low), (square, full), ((8, width), full)],
        inner_low,
        inner_all,
        grad_second,
        normed,
        recip,
        rows,
        w,
        query,
        key,
        value,
        context,
        attention,
        scratch_shapes=[pltpu.VMEM(square, low)],
    )
    bias_rows = (
        bias_sum.reshape(shards, spread, part).transpose(1, 0, 2).reshape(spread, width)
    )
    bias_rows = jnp.pad(bias_rows, ((0, 8 - spread), (0, 0)))
    own_block = scatter(
        swap_halves(*grad_block(x, context, grads, sums, more, bias_rows, part, core)), False
    )
    factor = float(x.shape[0] * lax.axis_size("rep") * shards) ** (-0.5)
    own_block = own_block * factor
    own = [own_block[:, i * width : (i + 1) * width] for i in range(4)]
    own_rows = own_block[:, 4 * width :].T
    return (
        block_rows.reshape(layer_input.shape),
        input_grad.reshape(layer_input.shape),
        own[0],
        own[1],
        own[2],
        own[3],
        own_rows[0],
        own_rows[1],
        own_rows[2],
        own_rows[3],
        own_rows[4],
        own_inner * factor,
        own_rows[16 : 16 + spread].reshape(-1),
        own_outer * factor,
        own_rows[8],
        own_rows[9],
        own_rows[10],
    )


def solution(mesh):
    placed = (
        P(("rep", "shard"), None, None),
        P(("rep", "shard")),
        P(("rep", "shard"), None, None),
        P("shard", None),
        P("shard", None),
        P("shard", None),
        P("shard", None),
        P("shard"),
        P("shard"),
        P("shard"),
        P("shard"),
        P("shard"),
        P("shard", None),
        P("shard"),
        P("shard", None),
        P("shard"),
        P("shard"),
        P("shard"),
    )
    return jax.shard_map(
        body,
        mesh=mesh,
        in_specs=placed,
        out_specs=(
            P(("rep", "shard"), None, None),
            P(("rep", "shard"), None, None),
            P("shard", None),
            P("shard", None),
            P("shard", None),
            P("shard", None),
            P("shard"),
            P("shard"),
            P("shard"),
            P("shard"),
            P("shard"),
            P("shard", None),
            P("shard"),
            P("shard", None),
            P("shard"),
            P("shard"),
            P("shard"),
        ),
        check_vma=False,
    )
```

```python
import functools

import jax
import jax.numpy as jnp
from jax import lax
from jax.experimental import pallas as pl
from jax.experimental.pallas import tpu as pltpu
from jax.sharding import PartitionSpec as P

HEAD_DIM = 64
LANES = 128


EPSILON = 1e-06
NEG_FILL = -1000000000.0
ROOT_HALF = 0.7071067811865476
INV_ROOT_TAU = 0.3989422804014327


def matmul(left, right):
    return jnp.dot(left, right, preferred_element_type=jnp.float32)


def transpose_left(left, right):
    return lax.dot_general(
        left, right, (((0,), (0,)), ((), ())), preferred_element_type=jnp.float32
    )


def transpose_right(left, right):
    return lax.dot_general(
        left, right, (((1,), (1,)), ((), ())), preferred_element_type=jnp.float32
    )


def row_mean(values):
    return jnp.mean(values, axis=-1, keepdims=True)


def norm_forward(hidden):
    center = hidden - row_mean(hidden)
    reciprocal = lax.rsqrt(row_mean(center * center) + EPSILON)
    return center * reciprocal, reciprocal


def norm_backward(upstream, normed, reciprocal, gain):
    scaled = upstream * gain
    return (scaled - row_mean(scaled) - normed * row_mean(scaled * normed)) * reciprocal


def column_sum(values):
    return jnp.sum(values, axis=0, keepdims=True)


def cost(micros):
    return pl.CostEstimate(
        flops=int(micros * 1e9), transcendentals=0, bytes_accessed=int(micros * 3e6)
    )


def call(kernel, micros, outs, gathered, *args, scratch=()):
    smem = pl.BlockSpec(memory_space=pltpu.SMEM)
    vmem = pl.BlockSpec(memory_space=pltpu.VMEM)
    apart = pl.BlockSpec(memory_space=pl.ANY)
    shard = lax.axis_index("shard").reshape(1)
    pieces = [piece for group, _ in gathered for piece in group]
    held = []
    for group, rels in gathered:
        count = sum(len(rel) for rel in rels)
        held.append(pltpu.VMEM((count,) + group[0].shape[1:], group[0].dtype))
        held.append(pltpu.SemaphoreType.DMA((count,)))

    def run(shard_ref, *refs):
        lefts, rest = refs[: len(pieces)], refs[len(pieces) :]
        rest, holders = rest[: len(rest) - len(held)], rest[len(rest) - len(held) :]
        loads, start = [], 0
        for i, (group, rels) in enumerate(gathered):
            loads.append(
                fetch(lefts[start : start + len(group)], rels, shard_ref[0], *holders[2 * i : 2 * i + 2])
            )
            start += len(group)
        kernel(*loads, *rest)

    return pl.pallas_call(
        run,
        out_shape=[jax.ShapeDtypeStruct(shape, dtype) for shape, dtype in outs],
        in_specs=[smem]
        + [apart] * len(pieces)
        + [smem if a.dtype == jnp.int32 else vmem for a in args],
        out_specs=[vmem] * len(outs),
        scratch_shapes=list(scratch) + held,
        cost_estimate=cost(micros),
        compiler_params=pltpu.CompilerParams(vmem_limit_bytes=60 << 20),
    )(shard, *pieces, *args)


def fetch(lefts, rels, shard, held, sems):
    copies = []
    for left, rel in zip(lefts, rels):
        for i, r in enumerate(rel):
            place = shard ^ r if len(rels) > 1 else r
            copies.append(
                pltpu.make_async_copy(left.at[i], held.at[place], sems.at[len(copies)])
            )
    for copy in copies:
        copy.start()

    def ready():
        for copy in copies:
            copy.wait()
        return held

    return ready


def columns(held, first, last):
    block = held[:, :, first:last]
    return block.reshape(-1, last - first)


def rows_of(held, first, last):
    part = held.shape[1]
    block = held[first // part : last // part]
    return block.reshape(last - first, held.shape[2])


def attention_forward(
    load, length, x, query, key, value, context, attention, low, normed, recip, rows
):
    width = x.shape[1]
    w = load()
    table = columns(w, 4 * width, 4 * width + LANES).astype(jnp.float32).T
    rows[...] = table[: rows.shape[0]]
    query[...] = (matmul(x[...], columns(w, 0, width)) + rows[0:1]).astype(jnp.bfloat16)
    key[...] = matmul(x[...], columns(w, width, 2 * width)).astype(jnp.bfloat16)
    value[...] = (matmul(x[...], columns(w, 2 * width, 3 * width)) + rows[1:2]).astype(jnp.bfloat16)
    count = x.shape[0]
    valid = lax.broadcasted_iota(jnp.int32, (count, count), 1) < length[0]
    lane = lax.broadcasted_iota(jnp.int32, (count, LANES), 1) // HEAD_DIM

    def pair(j, carry):
        at = pl.ds(pl.multiple_of(j * LANES, LANES), LANES)
        queries, keys, values = query[:, at], key[:, at], value[:, at]
        total = jnp.zeros((count, LANES), jnp.float32)
        for h in range(LANES // HEAD_DIM):
            mine = jnp.where(lane == h, queries, jnp.zeros_like(queries))
            scores = transpose_right(mine, keys) * HEAD_DIM ** (-0.5)
            scores = jnp.where(valid, scores, NEG_FILL)
            top = jnp.max(scores, axis=-1, keepdims=True)
            log_total = top + jnp.log(jnp.sum(jnp.exp(scores - top), axis=-1, keepdims=True))
            attend = jnp.exp(scores - log_total)
            first = pl.multiple_of((j * (LANES // HEAD_DIM) + h) * count, count)
            attention[pl.ds(first, count), :] = attend
            total = jnp.where(lane == h, matmul(attend.astype(jnp.bfloat16), values), total)
        context[:, at] = total.astype(jnp.bfloat16)
        return carry

    lax.fori_loop(0, width // LANES, pair, 0)
    first_sum = (
        x[...].astype(jnp.float32)
        + matmul(context[...], columns(w, 3 * width, 4 * width))
        + rows[2:3]
    )
    first_normed, first_recip = norm_forward(first_sum)
    normed[...] = first_normed
    recip[...] = jnp.broadcast_to(first_recip, recip.shape)
    low[...] = (first_normed * rows[3:4] + rows[4:5]).astype(jnp.bfloat16)


def inner_forward(load, low, bias, active, slope):
    chunk = 4 * LANES
    w = load()
    for start in range(0, bias.shape[1], chunk):
        at = slice(start, start + chunk)
        pre = matmul(low[...], columns(w, start, start + chunk)) + bias[:, at]
        half = 0.5 * (1.0 + lax.erf(pre * ROOT_HALF))
        active[:, at] = (pre * half).astype(jnp.bfloat16)
        slope[:, at] = half + pre * jnp.exp(-0.5 * pre * pre) * INV_ROOT_TAU


def outer_both(
    load, normed, rows, active, slope, upstream, block, grad, low, inner_low, sums, bias
):
    w = load()
    hidden = active.shape[1]
    first_out = normed[...] * rows[3:4] + rows[4:5]
    second_sum = first_out + matmul(active[...], rows_of(w, 0, hidden)) + rows[5:6]
    second_normed, second_recip = norm_forward(second_sum)
    block[...] = (second_normed * rows[6:7] + rows[7:8]).astype(jnp.bfloat16)
    above = upstream[...].astype(jnp.float32)
    grad_second = norm_backward(above, second_normed, second_recip, rows[6:7])
    grad[...] = grad_second
    low[...] = grad_second.astype(jnp.bfloat16)
    sums[...] = jnp.zeros_like(sums)
    sums[0:1] = column_sum(grad_second)
    sums[1:2] = column_sum(above * second_normed)
    sums[2:3] = column_sum(above)
    chunk = 3 * LANES
    for start in range(0, hidden, chunk):
        at = slice(start, start + chunk)
        grad_pre = transpose_right(low[...], rows_of(w, start, start + chunk)) * slope[:, at]
        inner_low[:, at] = grad_pre.astype(jnp.bfloat16)
        bias[:, at] = column_sum(grad_pre)


def attention_backward(
    load,
    inner_load,
    inner_low,
    grad_second,
    normed,
    recip,
    rows,
    query,
    key,
    value,
    context,
    attention,
    grads,
    input_grad,
    sums,
    context_low,
):
    count, width = normed.shape
    inner_w = inner_load()
    grad_out = (
        transpose_right(inner_low[...], columns(inner_w, 0, inner_w.shape[2])) + grad_second[...]
    )
    w = load()
    grad_first = norm_backward(grad_out, normed[...], recip[:, 0:1], rows[3:4])
    sums[...] = jnp.zeros_like(sums)
    sums[2:3] = column_sum(grad_first)
    sums[3:4] = column_sum(grad_out * normed[...])
    sums[4:5] = column_sum(grad_out)
    grads[3] = grad_first.astype(jnp.bfloat16)
    context_low[...] = transpose_right(
        grads[3], columns(w, 3 * width, 4 * width)
    ).astype(jnp.bfloat16)
    lane = lax.broadcasted_iota(jnp.int32, (count, LANES), 1) // HEAD_DIM

    def pair(j, carry):
        at = pl.ds(pl.multiple_of(j * LANES, LANES), LANES)
        queries, keys, values = query[:, at], key[:, at], value[:, at]
        above = context_low[:, at]
        both = above.astype(jnp.float32) * context[:, at].astype(jnp.float32)
        total = [jnp.zeros((count, LANES), jnp.float32)] * 3
        for h in range(LANES // HEAD_DIM):
            mine = lane == h
            first = pl.multiple_of((j * (LANES // HEAD_DIM) + h) * count, count)
            attend = attention[pl.ds(first, count), :]
            grad_attend = transpose_right(jnp.where(mine, above, jnp.zeros_like(above)), values)
            across = jnp.sum(jnp.where(mine, both, 0.0), axis=-1, keepdims=True)
            score = (attend * (grad_attend - across) * HEAD_DIM ** (-0.5)).astype(jnp.bfloat16)
            parts = [
                matmul(score, keys),
                transpose_left(score, queries),
                transpose_left(attend.astype(jnp.bfloat16), above),
            ]
            total = [jnp.where(mine, new, old) for new, old in zip(parts, total)]
        for i in range(3):
            grads[i, :, at] = total[i].astype(jnp.bfloat16)
        sums[0:1, at] = column_sum(total[0])
        sums[1:2, at] = column_sum(total[2])
        return carry

    lax.fori_loop(0, width // LANES, pair, 0)
    result = grad_first
    for i in range(3):
        result += transpose_right(grads[i], columns(w, i * width, (i + 1) * width))
    input_grad[...] = result


def split_halves(core, block, scratch, send, keep, part, at):
    scratch[...] = block
    for i in range(block.shape[0] // (2 * part)):
        base = 2 * part * i
        theirs = pl.ds(pl.multiple_of(base + (1 - core) * part, 8), part)
        ours = pl.ds(pl.multiple_of(base + core * part, 8), part)
        send[i * part : (i + 1) * part, at] = scratch[theirs, :].astype(jnp.bfloat16)
        keep[i * part : (i + 1) * part, at] = scratch[ours, :]


def weight_grad(part, core, left, right, send, keep, scratch):
    total = transpose_left(left[...], right[...])
    split_halves(core[0], total, scratch, send, keep, part, slice(0, right.shape[1]))


def block_grad(part, core, x, context, grads, sums, more, bias, send, keep, scratch, thin):
    width = grads.shape[2]
    for i in range(4):
        left = context if i == 3 else x
        total = transpose_left(left[...], grads[i])
        at = slice(i * width, (i + 1) * width)
        split_halves(core[0], total, scratch, send, keep, part, at)
    table = jnp.concatenate([sums[...], more[...], bias[...]], axis=0)
    table = jnp.concatenate(
        [table, jnp.zeros((LANES - table.shape[0], table.shape[1]), jnp.float32)], axis=0
    )
    split_halves(
        core[0], table.T, thin, send, keep, part, slice(4 * width, 4 * width + LANES)
    )


def swap(values, axis, bit):
    pairs = [(i, i ^ bit) for i in range(lax.axis_size(axis))]
    return lax.ppermute(values, axis, pairs)


def has_bit(axis, bit):
    return (lax.axis_index(axis) & bit) != 0


def bits_of(axis):
    return [1 << k for k in range(lax.axis_size(axis).bit_length() - 1)]


def after(value, *others):
    return lax.optimization_barrier((value,) + others)[0]


def far_stage(block, waits):
    bits = bits_of("shard")
    held, rel = block[None], [0]
    for bit in bits[:2:-1]:
        other = swap(after(held, *waits), "shard", bit)
        held, rel, waits = jnp.concatenate([held, other]), rel + [r ^ bit for r in rel], []
    return held, rel, other


def near_stage(held, rel, first_waits, second_waits, last_waits):
    bits = bits_of("shard")
    more = swap(held, "shard", bits[2])
    first = swap(after(held, *first_waits), "shard", bits[1])
    second = swap(after(more, *second_waits), "shard", bits[1])
    rel = rel + [r ^ bits[2] for r in rel]
    mine = jnp.concatenate([held, more])
    yours = jnp.concatenate([first, second])
    pieces = [mine, yours, swap(mine, "shard", 1), swap(after(yours, *last_waits), "shard", 1)]
    rels = [[r ^ bit for r in rel] for bit in (0, bits[1], 1, bits[1] ^ 1)]
    if mine.shape[1] % 16:
        stacked = jnp.concatenate(pieces)
        order = jnp.argsort(jnp.asarray(sum(rels, [])) ^ lax.axis_index("shard"))
        stacked = jnp.take(stacked, order, axis=0)
        pieces = [stacked.reshape(1, -1, stacked.shape[2])]
        rels = [[0]]
    return (pieces, rels), first, second


def halve(total, axis, bit, before):
    columns = total.shape[-1]
    mine = has_bit(axis, bit).astype(jnp.int32)
    total = total.reshape(before, 2, -1, columns)
    send = lax.dynamic_index_in_dim(total, 1 - mine, 1, keepdims=False)
    keep = lax.dynamic_index_in_dim(total, mine, 1, keepdims=False)
    send, keep = send.reshape(-1, columns), keep.reshape(-1, columns)
    other = swap(send.astype(jnp.bfloat16), axis, bit)
    return keep.astype(jnp.float32) + other.astype(jnp.float32)


def scatter(total, rep_first):
    bits, reps = bits_of("shard"), bits_of("rep")
    columns = total.shape[-1]
    left = [("shard", bit) for bit in reversed(bits[1:])] + [("rep", bit) for bit in reversed(reps)]
    across = [("rep", bit) for bit in reps]
    near = [("shard", bit) for bit in bits[1:2]]
    order = across + near if rep_first else near + across
    order += [("shard", bit) for bit in bits[2:]]
    for step in order:
        place = left.index(step)
        total = halve(total, step[0], step[1], 1 << place)
        left.pop(place)
    for bit in reps:
        other = swap(total.astype(jnp.bfloat16), "rep", bit).astype(jnp.float32)
        high = has_bit("rep", bit)
        total = jnp.concatenate(
            [jnp.where(high, other, total), jnp.where(high, total, other)], axis=0
        )
    return total


def swap_halves(send, keep):
    other = swap(send, "shard", 1)
    return keep + other.astype(jnp.float32)


def grad_pair(left, right, part, core):
    count, rows = left.shape
    columns = right.shape[1]
    step, wide = 3 * LANES, 6 * LANES
    return pl.pallas_call(
        functools.partial(weight_grad, part),
        grid=(rows // step, columns // wide),
        in_specs=[
            pl.BlockSpec(memory_space=pltpu.SMEM),
            pl.BlockSpec((count, step), lambda i, j: (0, i)),
            pl.BlockSpec((count, wide), lambda i, j: (0, j)),
        ],
        out_specs=[pl.BlockSpec((step // 2, wide), lambda i, j: (i, j))] * 2,
        out_shape=[
            jax.ShapeDtypeStruct((rows // 2, columns), jnp.bfloat16),
            jax.ShapeDtypeStruct((rows // 2, columns), jnp.float32),
        ],
        scratch_shapes=[pltpu.VMEM((step, wide), jnp.float32)],
        cost_estimate=cost(8),
    )(core, left, right)


def grad_block(x, context, grads, sums, more, bias, part, core):
    count, width = x.shape
    step = 3 * LANES
    columns = 4 * width + LANES
    thin = pl.BlockSpec((8, step), lambda i: (0, i))
    return pl.pallas_call(
        functools.partial(block_grad, part),
        grid=(width // step,),
        in_specs=[
            pl.BlockSpec(memory_space=pltpu.SMEM),
            pl.BlockSpec((count, step), lambda i: (0, i)),
            pl.BlockSpec((count, step), lambda i: (0, i)),
            pl.BlockSpec((4, count, width), lambda i: (0, 0, 0)),
            thin,
            thin,
            thin,
        ],
        out_specs=[pl.BlockSpec((step // 2, columns), lambda i: (i, 0))] * 2,
        out_shape=[
            jax.ShapeDtypeStruct((width // 2, columns), jnp.bfloat16),
            jax.ShapeDtypeStruct((width // 2, columns), jnp.float32),
        ],
        scratch_shapes=[
            pltpu.VMEM((step, width), jnp.float32),
            pltpu.VMEM((step, LANES), jnp.float32),
        ],
        cost_estimate=cost(6),
    )(core, x, context, grads, sums, more, bias)


def body(
    layer_input,
    lengths,
    cotangent,
    query_weight,
    key_weight,
    value_weight,
    output_weight,
    query_bias,
    value_bias,
    output_bias,
    first_gain,
    first_shift,
    inner_weight,
    inner_bias,
    outer_weight,
    outer_bias,
    second_gain,
    second_shift,
):
    count, width = layer_input.shape[1:]
    x = layer_input.reshape(-1, width)
    part, hidden = query_weight.shape[0], inner_weight.shape[1]
    shards = lax.axis_size("shard")
    spread = inner_bias.shape[0] // part
    vectors = [
        query_bias,
        value_bias,
        output_bias,
        first_gain,
        first_shift,
        outer_bias,
        second_gain,
        second_shift,
    ]
    table = jnp.concatenate(
        [jnp.stack(vectors), inner_bias.reshape(spread, part)], axis=0
    )
    table = jnp.pad(table.T, ((0, 0), (0, LANES - table.shape[0])))
    attention_block = jnp.concatenate(
        [query_weight, key_weight, value_weight, output_weight, table], axis=1
    )
    low, full = jnp.bfloat16, jnp.float32
    heads = width // HEAD_DIM
    square = (count, width)
    held, rel, far = far_stage(attention_block, [])
    w, first, second = near_stage(held, rel, [], [], [])
    held, rel, far = far_stage(inner_weight, [far])
    inner_all, first, second = near_stage(held, rel, [first], [second], [])
    query, key, value, context, attention, first_low, normed, recip, rows = call(
        attention_forward,
        12,
        [(square, low)] * 4
        + [((heads * count, count), full), (square, low), (square, full)]
        + [((count, LANES), full), ((16, width), full)],
        [w],
        lengths,
        x,
    )
    bias = rows[8 : 8 + spread].reshape(spread, shards, part).transpose(1, 0, 2).reshape(1, -1)
    active, slope = call(
        inner_forward,
        7,
        [((count, hidden), low), ((count, hidden), full)],
        [inner_all],
        first_low,
        bias,
    )
    held, rel, far = far_stage(outer_weight, [far])
    outer_all, first, second = near_stage(held, rel, [first, first_low], [second], [active])
    block_rows, grad_second, second_low, inner_low, more, bias_sum = call(
        outer_both,
        9,
        [
            (square, low),
            (square, full),
            (square, low),
            ((count, hidden), low),
            ((8, width), full),
            ((1, hidden), full),
        ],
        [outer_all],
        normed,
        rows,
        active,
        slope,
        cotangent.reshape(-1, width),
    )
    core = (lax.axis_index("shard") & 1).reshape(1)
    own_outer = scatter(swap_halves(*grad_pair(active, second_low, part * spread, core)), True)
    own_inner = scatter(swap_halves(*grad_pair(first_low, inner_low, part, core)), False)
    grads, input_grad, sums = call(
        attention_backward,
        16,
        [((4,) + square, low), (square, full), ((8, width), full)],
        [w, inner_all],
        inner_low,
        grad_second,
        normed,
        recip,
        rows,
        query,
        key,
        value,
        context,
        attention,
        scratch=[pltpu.VMEM(square, low)],
    )
    bias_rows = (
        bias_sum.reshape(shards, spread, part).transpose(1, 0, 2).reshape(spread, width)
    )
    bias_rows = jnp.pad(bias_rows, ((0, 8 - spread), (0, 0)))
    own_block = scatter(
        swap_halves(*grad_block(x, context, grads, sums, more, bias_rows, part, core)), False
    )
    factor = float(x.shape[0] * lax.axis_size("rep") * shards) ** (-0.5)
    own_block = own_block * factor
    own = [own_block[:, i * width : (i + 1) * width] for i in range(4)]
    own_rows = own_block[:, 4 * width :].T
    return (
        block_rows.reshape(layer_input.shape),
        input_grad.reshape(layer_input.shape),
        own[0],
        own[1],
        own[2],
        own[3],
        own_rows[0],
        own_rows[1],
        own_rows[2],
        own_rows[3],
        own_rows[4],
        own_inner * factor,
        own_rows[16 : 16 + spread].reshape(-1),
        own_outer * factor,
        own_rows[8],
        own_rows[9],
        own_rows[10],
    )


def solution(mesh):
    placed = (
        P(("rep", "shard"), None, None),
        P(("rep", "shard")),
        P(("rep", "shard"), None, None),
        P("shard", None),
        P("shard", None),
        P("shard", None),
        P("shard", None),
        P("shard"),
        P("shard"),
        P("shard"),
        P("shard"),
        P("shard"),
        P("shard", None),
        P("shard"),
        P("shard", None),
        P("shard"),
        P("shard"),
        P("shard"),
    )
    return jax.shard_map(
        body,
        mesh=mesh,
        in_specs=placed,
        out_specs=(
            P(("rep", "shard"), None, None),
            P(("rep", "shard"), None, None),
            P("shard", None),
            P("shard", None),
            P("shard", None),
            P("shard", None),
            P("shard"),
            P("shard"),
            P("shard"),
            P("shard"),
            P("shard"),
            P("shard", None),
            P("shard"),
            P("shard", None),
            P("shard"),
            P("shard"),
            P("shard"),
        ),
        check_vma=False,
    )
```
